128 devices in a mesh: mode: 32 (over x, y, core), wall: 2 (over z_lo), ckpt: 2 (over z_hi).
Axes of the slice: x: 4, y: 4, z: 4 (z_hi: 2, z_lo: 2; z = z_hi * 2 + z_lo), core: 2. Of those that a mesh axis runs over, the one named last changes fastest.
Arguments:
- adjoint: float32 [2, 5, 1024, 4096], P(None, None, ('wall', 'ckpt'), 'mode'), may hold values from -6 to 6
- forward: float32 [2, 2, 1024, 4096], P('ckpt', None, 'wall', 'mode'), may hold values from -0.09375 to 0.09375
- mode_map: int32 [4096], P('mode'), may hold values from 0 to 4095, as said below
Outputs:
- adjoint_prev: float32 [2, 5, 1024, 4096], P(None, None, ('wall', 'ckpt'), 'mode')
The draws below stay inside these ranges and needn't reach their ends.
Inputs may be any that keep to these rules, and one draw needn't show every extreme that they name: mode_map is a permutation of the 64 x 64 modes laid out by frequency: for every block b of 64 consecutive slots there is a frequency p(b) such that slot b * 64 + r holds mode p(b) * 64 + r, and p takes every frequency once.
All inputs are finite; a program needn't handle non-finite values.
Results may differ from the reference program's by a relative error of at most 0.0001.
Values sent between devices are 32-bit elements; how exact they have to be, the bound alone decides.
A program may use at most 128 MiB of HBM per device.

```python
import math
import jax
import jax.numpy as jnp
from jax import lax

NF = 64
NK = 64
FIELDS = 5
MODES = 4096
NY = 1024
STATIONS = 2


def draw_mode_map(key, part):
    freq_order = jax.random.permutation(jax.random.fold_in(key, 11), NF).astype(jnp.int32)
    span_ids = jnp.arange(NK, dtype=jnp.int32)
    return (freq_order[:, None] * NK + span_ids[None, :]).reshape(MODES).astype(jnp.int32)


def block_levels(own_key, shape, shards, smallest, largest):
    def one(position, blocks):
        steps = jax.random.uniform(jax.random.fold_in(jax.random.fold_in(own_key, 6), position), (blocks,), jnp.float32, smallest / len(shards), largest / len(shards))
        return jnp.repeat(jnp.exp(steps), shape[position] // blocks).reshape((-1,) + (1,) * (len(shape) - position - 1))

    loudness = one(*shards[0])
    for cut in shards[1:]:
        loudness = loudness * one(*cut)
    return loudness


def centred(rng, dims, width, reach, cuts=(), held_as=jnp.bfloat16):
    level = block_levels(rng, dims, cuts, -0.22, 0.18) if cuts else 1.0
    values = jax.random.normal(rng, dims, jnp.float32) * width * level
    return jnp.minimum(jnp.maximum(values, -reach), reach).astype(held_as)


def setup_inputs(seed: int = 0) -> dict:
    splits = jax.random.split(jax.random.key(seed), 4)
    return {
        "adjoint": centred(splits[0], (2, FIELDS, NY, MODES), 1.0, 6.0, ((2, 4), (3, 32)), jnp.float32),
        "forward": centred(splits[1], (STATIONS, 2, NY, MODES), MODES ** -0.5, 0.09375, ((0, 2), (2, 2), (3, 32)), jnp.float32),
        "mode_map": draw_mode_map(jax.random.fold_in(splits[3], 71), 0),
    }


def rates(grid_index):
    freq_index = grid_index // NK
    span_index = grid_index % NK
    freq_signed = (freq_index + NF // 2) % NF - NF // 2
    span_signed = (span_index + NK // 2) % NK - NK // 2
    return (2.0 / NF * freq_signed.astype(jnp.float32), 2.0 / NK * span_signed.astype(jnp.float32))

def reference(adjoint, forward, mode_map):
    slot_index = mode_map.astype(jnp.int32)
    placed = jnp.zeros((MODES,), jnp.int32).at[slot_index].set(jnp.arange(MODES, dtype=jnp.int32))
    alpha_rate, beta_rate = rates(slot_index)

    def to_phys(real_part, imag_part):
        joined = lax.complex(real_part, imag_part)[..., placed]
        joined = joined.reshape(joined.shape[:-1] + (NF, NK))
        return jnp.fft.ifft2(joined) * (NF * NK)

    def to_modes(product):
        spectrum = jnp.fft.fft2(product) / (NF * NK)
        spectrum = spectrum.reshape(spectrum.shape[:-2] + (MODES,))[..., slot_index]
        return (jnp.real(spectrum), jnp.imag(spectrum))
    row_scale = 1.0 / math.sqrt(NY)
    current = adjoint
    for station in range(STATIONS - 1, -1, -1):
        forward_phys = to_phys(forward[station, 0], forward[station, 1])
        adjoint_phys = to_phys(current[0], current[1])
        product = jnp.conj(forward_phys)[None] * adjoint_phys
        coupled_real, coupled_imag = to_modes(product)
        coupled = jnp.stack([coupled_real, coupled_imag])
        zero_row = jnp.zeros_like(current[:, :, :1])
        above_rows = jnp.concatenate([current[:, :, 1:], zero_row], 2)
        below_rows = jnp.concatenate([zero_row, current[:, :, :-1]], 2)
        stepped = current + 0.2 * (above_rows - 2.0 * current + below_rows) - 0.5 * coupled
        running_real = jnp.cumsum(alpha_rate * stepped[0, 0] + beta_rate * stepped[0, 2], axis=0)
        running_imag = jnp.cumsum(alpha_rate * stepped[1, 0] + beta_rate * stepped[1, 2], axis=0)
        stepped = stepped.at[0, 1].add(running_imag * row_scale)
        stepped = stepped.at[1, 1].add(-running_real * row_scale)
        current = stepped
    return current
```

```python
import functools

import jax
import jax.numpy as jnp
import numpy as np
from jax import lax
from jax.experimental import pallas as pl
from jax.experimental.pallas import tpu as pltpu
from jax.sharding import PartitionSpec as P

NF = 64
NK = 64
NY = 1024
PEERS = 32
ROWS = 256
F32 = jnp.float32
BF16 = jnp.bfloat16
MESH = pl.DeviceIdType.MESH

IN = {2: 0, 0: 1, 3: 3, 4: 5, 1: 6}
F_OWN, F_OTHER, MID, BACK = 2, 4, 7, 8
OUT = {0: 9, 2: 10, 3: 11, 4: 12, 1: 13}
SLOTS = 14


def hi_lo(table):
    hi = table.astype(np.float32).astype(BF16)
    lo = (table - hi.astype(np.float64)).astype(np.float32).astype(BF16)
    return jnp.asarray(hi), jnp.asarray(lo)


def complex_blocks(cosine, sine):
    return np.stack([np.stack([cosine, -sine]), np.stack([sine, cosine])])


def tables():
    ids = np.arange(64)
    angle = 2.0 * np.pi / 64 * (ids[:, None] * ids[None, :] % 64)
    cosine, sine = np.cos(angle), np.sin(angle)
    blocks = complex_blocks(cosine, sine)
    eye = np.eye(2)
    span = np.einsum("pqzk,ab->zpaqbk", blocks, eye).reshape(256, 256)
    time = np.einsum("pqtg,ab->patbqg", blocks, eye).reshape(256, 256)
    signed = (ids + 32) % 64 - 32
    beta = 2.0 * signed / 64
    lag = ids[:, None] - ids[None, :]
    wave = np.exp(2j * np.pi / 64 * (lag[:, :, None] * ids % 64))
    slope = (-1j / np.sqrt(NY)) * (wave * beta).sum(-1) / 64
    deriv = np.einsum(
        "pqzx,ab->zpaxqb", complex_blocks(slope.real, slope.imag), eye
    ).reshape(256, 256)
    upto = (np.arange(256)[:, None] <= np.arange(256)[None, :]).astype(np.float32)
    return (
        *hi_lo(span),
        *hi_lo(time),
        *hi_lo(-time.T / 128),
        *hi_lo(deriv),
        jnp.asarray(upto.astype(BF16)),
        jnp.asarray(upto.T.astype(BF16)),
    )


def split(x):
    hi = x.astype(BF16)
    return hi, (x - hi.astype(F32)).astype(BF16)


def dot(a, b, ca=1, cb=0):
    return lax.dot_general(a, b, (((ca,), (cb,)), ((), ())), preferred_element_type=F32)


def kernel(
    map_s, map_v, adj, fwd, span_h, span_l, time_h, time_l, inv_h, inv_l, der_h, der_l,
    upper, lower, out,
    xin, fin, fz, ptile, ptab, sb, db, es, eh, tb, ft, ftb, tm, ti, amp, phys, qs, stage,
    load_sem, fload_sem, fz_sem, p_sem, ssem, rsem, es_sem, er_sem, tt_sem, ft_sem, st_sem,
):
    me = lax.axis_index("mode")
    wall, ckpt = lax.axis_index("wall"), lax.axis_index("ckpt")
    mx, my, mc = me // 8, (me // 2) % 4, me % 2
    rank = wall * 2 + ckpt

    def peer(i):
        return ((mx + i // 8) % 4) * 8 + ((my + (i // 2) % 4) % 4) * 2 + (mc + i % 2) % 2

    def plane(offset):
        other = (rank + offset) % 4
        return {"wall": other // 2, "ckpt": other % 2}

    bar = pltpu.get_barrier_semaphore()

    def greet(i, carry):
        pl.semaphore_signal(bar, inc=1, device_id={"mode": peer(i)}, device_id_type=MESH)
        return carry

    lax.fori_loop(1, PEERS, greet, 0)
    for o in (1, 2, 3):
        pl.semaphore_signal(bar, inc=1, device_id=plane(o), device_id_type=MESH)

    loads = {}
    for c in (2, 0, 3, 4, 1):
        loads[c] = pltpu.make_async_copy(adj.at[:, c], xin.at[c], load_sem.at[c])
        loads[c].start()
    load_f = pltpu.make_async_copy(
        fwd.at[0, :, pl.ds(ckpt * ROWS, ROWS)], fin, fload_sem
    )
    load_f.start()

    row8 = lax.broadcasted_iota(jnp.int32, (8, 128), 0)
    ptile[...] = jnp.where(row8 % 2 == 0, map_s[0, 0] >> 6, map_s[0, 64] >> 6)

    pl.semaphore_wait(bar, PEERS - 1 + 3)

    send_fz = pltpu.make_async_remote_copy(
        fwd.at[0, :, pl.ds((1 - ckpt) * ROWS, ROWS)], fz, fz_sem.at[0], fz_sem.at[1],
        device_id={"ckpt": 1 - ckpt}, device_id_type=MESH,
    )
    send_fz.start()

    def send_p(i, carry):
        p = peer(i)
        pltpu.make_async_remote_copy(
            ptile, ptab.at[me], p_sem.at[0], p_sem.at[1],
            device_id={"mode": p}, device_id_type=MESH,
        ).start()
        return carry

    lax.fori_loop(1, PEERS, send_p, 0)
    ptab[me] = ptile[...]

    def exchange(k, value):
        sb[k] = value.reshape(PEERS, 8, ROWS)

        def one(i, carry):
            p = peer(i)
            pltpu.make_async_remote_copy(
                sb.at[k, p], db.at[k, me], ssem.at[k], rsem.at[k],
                device_id={"mode": p}, device_id_type=MESH,
            ).start()
            return carry

        lax.fori_loop(1, PEERS, one, 0)
        db[k, me] = sb[k, me]

    def whole(k):
        n = pl.ds(0, PEERS - 1)
        return pltpu.make_async_remote_copy(
            sb.at[k, n], db.at[k, n], ssem.at[k], rsem.at[k],
            device_id={"mode": peer(1)}, device_id_type=MESH,
        )

    def arrived(k):
        whole(k).wait_recv()
        return db[k].reshape(ROWS, ROWS)

    def dot3(ah, al, x, cb=0):
        xh, xl = split(x)
        return dot(ah[...], xh, 1, cb) + dot(ah[...], xl, 1, cb) + dot(al[...], xh, 1, cb)

    def to_span(real, imag):
        return dot3(span_h, span_l, jnp.concatenate([real, imag], 1), 1)

    def send_field(c):
        loads[c].wait()
        exchange(IN[c], to_span(xin[c, 0], xin[c, 1]))

    send_field(2)
    send_field(0)
    load_f.wait()
    exchange(F_OWN, to_span(fin[0], fin[1]))
    send_field(3)

    n = pl.ds(0, PEERS - 1)
    wait_p = pltpu.make_async_remote_copy(
        ptab.at[n], ptab.at[n], p_sem.at[0], p_sem.at[1],
        device_id={"mode": peer(1)}, device_id_type=MESH,
    )
    wait_p.wait_recv()
    freq = ptab[...].reshape(ROWS, 128)
    row = lax.broadcasted_iota(jnp.int32, (ROWS, 128), 0)
    lane = lax.broadcasted_iota(jnp.int32, (ROWS, 128), 1)
    inside = (row % 8) // 2
    onehot = jnp.concatenate(
        [
            jnp.where(inside * 64 + freq == lane + half * 128, 1.0, 0.0)
            for half in (0, 1)
        ],
        1,
    ).astype(BF16)
    tm[0] = dot(time_h[...], onehot, 1, 1).astype(BF16)
    tm[1] = dot(time_l[...], onehot, 1, 1).astype(BF16)
    ti[0] = dot(onehot, inv_h[...]).astype(BF16)
    ti[1] = dot(onehot, inv_l[...]).astype(BF16)
    signed = jnp.where(freq >= 32, freq - 64, freq).astype(F32) * (1.0 / 1024)
    amp[...] = jnp.where((row // 2) % 2 == 0, signed, -signed)

    first, last = lane == 0, lane == 127
    has_low = (rank > 0).astype(F32)
    has_high = (rank < 3).astype(F32)

    def edge_copies(j):
        return [
            pltpu.make_async_remote_copy(
                es.at[j, s], eh.at[j, s], es_sem.at[j, s], er_sem.at[j, s],
                device_id=plane(o), device_id_type=MESH,
            )
            for s, o in ((0, 1), (1, 3))
        ]

    def send_edges(j, x):
        comb = jnp.where(
            last,
            pltpu.roll(x[:, :128], 127, 1),
            jnp.where(first, pltpu.roll(x[:, 128:], 1, 1), 0.0),
        ).T
        es[j, 0] = comb[:8]
        es[j, 1] = comb[120:]
        for copy in edge_copies(j):
            copy.start()

    def smoothed(x, low, high):
        halo = jnp.concatenate([low, jnp.zeros((112, ROWS), F32), high]).T
        xl, xh = x[:, :128], x[:, 128:]
        dl, dh = pltpu.roll(xl, 1, 1), pltpu.roll(xh, 1, 1)
        ul, uh = pltpu.roll(xl, 127, 1), pltpu.roll(xh, 127, 1)
        below = jnp.concatenate([jnp.where(first, halo, dl), jnp.where(first, dl, dh)], 1)
        above = jnp.concatenate([jnp.where(last, uh, ul), jnp.where(last, halo, uh)], 1)
        return x + 0.2 * ((above - 2.0 * x) + below)

    def to_time(x):
        return dot3(tm.at[0], tm.at[1], x)

    def prepare(c, x, j):
        send_edges(j, x)
        amp_phys = to_time(x)
        phys[c] = amp_phys

    def coupled(c, s):
        ar, ai = phys[c, :128], phys[c, 128:]
        fr, fi = phys[5 + s, :128], phys[5 + s, 128:]
        prod = jnp.concatenate([fr * ar + fi * ai, fr * ai - fi * ar])
        return dot3(ti.at[0], ti.at[1], prod)

    def step(c, x, s, j):
        term = coupled(c, s)
        for copy in edge_copies(j):
            copy.wait_recv()
        return smoothed(x, eh[j, 0] * has_low, eh[j, 1] * has_high) + term

    def first_step(c):
        qs[c] = step(c, db[IN[c]].reshape(ROWS, ROWS), 1, c)

    def begin(c):
        prepare(c, arrived(IN[c]), c)

    def again(c):
        prepare(c, qs[c], 5 + c)

    def finish(c):
        exchange(OUT[c], step(c, qs[c], 0, 5 + c))

    begin(2)
    begin(0)
    send_fz.wait_recv()
    exchange(F_OTHER, to_span(fz[0], fz[1]))
    send_field(4)
    send_field(1)
    phys[5 + ckpt] = to_time(arrived(F_OWN))
    begin(3)
    phys[6 - ckpt] = to_time(arrived(F_OTHER))
    first_step(2)
    exchange(MID, qs[2])
    first_step(0)
    again(0)
    again(2)
    begin(4)
    finish(0)
    first_step(3)
    again(3)
    finish(2)
    exchange(BACK, dot3(der_h, der_l, arrived(MID)))
    first_step(4)
    again(4)
    begin(1)
    first_step(1)
    finish(3)
    finish(4)

    u1 = qs[0]
    row2 = lax.broadcasted_iota(jnp.int32, (ROWS, ROWS), 0)
    turned = jnp.where(
        (row2 // 2) % 2 == 0, pltpu.roll(u1, ROWS - 2, 0), pltpu.roll(u1, 2, 0)
    )
    source = turned * jnp.concatenate([amp[...], amp[...]], 1) + arrived(BACK)
    sh, sl = split(source)
    running = dot(sh, upper[...]) + dot(sl, upper[...])
    v1 = qs[1] + running
    j = 6
    second = lane == 1
    comb = jnp.where(
        last,
        pltpu.roll(v1[:, :128], 127, 1),
        jnp.where(
            first,
            pltpu.roll(v1[:, 128:], 1, 1),
            jnp.where(second, pltpu.roll(running[:, 128:], 2, 1), 0.0),
        ),
    ).T
    es[j, 0] = comb[:8]
    es[j, 1] = comb[120:]
    for copy in edge_copies(j):
        copy.start()
    totals = [
        pltpu.make_async_remote_copy(
            es.at[j, 0], tb.at[o - 2], tt_sem.at[0, o - 2], tt_sem.at[1, o - 2],
            device_id=plane(o), device_id_type=MESH,
        )
        for o in (2, 3)
    ]
    for copy in totals:
        copy.start()
    mine = comb[:8]
    for copy in edge_copies(j) + totals:
        copy.wait_recv()
    nearest = eh[j, 0] * has_low
    beyond = tb[0] * (rank > 1).astype(F32) + tb[1] * (rank > 2).astype(F32)
    prefix = (nearest + beyond)[1:2]
    low = nearest + beyond[1:2] * has_low
    high = (eh[j, 1] + (prefix + mine[1:2])) * has_high
    column = jnp.concatenate([jnp.broadcast_to(prefix, (128, ROWS))]).T
    v1 = v1 + jnp.concatenate([column, column], 1)
    phys[1] = to_time(v1)
    exchange(OUT[1], smoothed(v1, low, high) + coupled(1, 0))

    def stores(c):
        return pltpu.make_async_copy(stage.at[:, c], out.at[:, c], st_sem.at[c])

    def to_slots(c):
        xh, xl = split(arrived(OUT[c]))
        return (
            dot(xh, span_h[...], 0, 0) + dot(xl, span_h[...], 0, 0) + dot(xh, span_l[...], 0, 0)
        ) * (1.0 / 64)

    def put(c, x):
        stage[0, c] = x[:, :128]
        stage[1, c] = x[:, 128:]
        stores(c).start()

    u0 = to_slots(0)
    put(0, u0)
    w0 = to_slots(2)
    put(2, w0)
    slot = map_v[...]
    fi, ki = slot >> 6, slot & 63
    alpha = jnp.where(fi >= 32, fi - 64, fi).astype(F32) * (1.0 / 1024)
    beta = jnp.where(ki >= 32, ki - 64, ki).astype(F32) * (1.0 / 1024)
    source = jnp.concatenate(
        [
            alpha * u0[:, 128:] + beta * w0[:, 128:],
            -(alpha * u0[:, :128] + beta * w0[:, :128]),
        ],
        1,
    )
    sh, sl = split(source)
    running = dot(lower[...], sh) + dot(lower[...], sl)
    ft[...] = running[248:]
    finals = [
        pltpu.make_async_remote_copy(
            ft, ftb.at[o - 1], ft_sem.at[0, o - 1], ft_sem.at[1, o - 1],
            device_id=plane(o), device_id_type=MESH,
        )
        for o in (1, 2, 3)
    ]
    for copy in finals:
        copy.start()
    put(3, to_slots(3))
    put(4, to_slots(4))
    for copy in finals:
        copy.wait_recv()
    total = (
        ftb[0] * has_low + ftb[1] * (rank > 1).astype(F32) + ftb[2] * (rank > 2).astype(F32)
    )[7:8]
    running = running + total
    put(1, to_slots(1) + running)

    for c in range(5):
        stores(c).wait()
    send_fz.wait_send()
    wait_p.wait_send()
    for k in range(SLOTS):
        whole(k).wait_send()
    for j in range(10):
        for copy in edge_copies(j):
            copy.wait_send()
    for copy in totals + finals:
        copy.wait_send()


def solution(mesh):
    def on_device(adjoint, forward, mode_map):
        slots = mode_map.reshape(1, 128)
        consts = tables()
        vmem = pl.BlockSpec(memory_space=pltpu.VMEM)
        anywhere = pl.BlockSpec(memory_space=pl.ANY)
        return pl.pallas_call(
            kernel,
            out_shape=jax.ShapeDtypeStruct(adjoint.shape, F32),
            in_specs=[pl.BlockSpec(memory_space=pltpu.SMEM), vmem, anywhere, anywhere]
            + [vmem] * len(consts),
            out_specs=anywhere,
            scratch_shapes=[
                pltpu.VMEM((5, 2, ROWS, 128), F32),
                pltpu.VMEM((2, ROWS, 128), F32),
                pltpu.VMEM((2, ROWS, 128), F32),
                pltpu.VMEM((8, 128), jnp.int32),
                pltpu.VMEM((PEERS, 8, 128), jnp.int32),
                pltpu.VMEM((SLOTS, PEERS, 8, ROWS), F32),
                pltpu.VMEM((SLOTS, PEERS, 8, ROWS), F32),
                pltpu.VMEM((10, 2, 8, ROWS), F32),
                pltpu.VMEM((10, 2, 8, ROWS), F32),
                pltpu.VMEM((2, 8, ROWS), F32),
                pltpu.VMEM((8, ROWS), F32),
                pltpu.VMEM((3, 8, ROWS), F32),
                pltpu.VMEM((2, ROWS, ROWS), BF16),
                pltpu.VMEM((2, ROWS, ROWS), BF16),
                pltpu.VMEM((ROWS, 128), F32),
                pltpu.VMEM((7, ROWS, ROWS), F32),
                pltpu.VMEM((5, ROWS, ROWS), F32),
                pltpu.VMEM((2, 5, ROWS, 128), F32),
                pltpu.SemaphoreType.DMA((5,)),
                pltpu.SemaphoreType.DMA,
                pltpu.SemaphoreType.DMA((2,)),
                pltpu.SemaphoreType.DMA((2,)),
                pltpu.SemaphoreType.DMA((SLOTS,)),
                pltpu.SemaphoreType.DMA((SLOTS,)),
                pltpu.SemaphoreType.DMA((10, 2)),
                pltpu.SemaphoreType.DMA((10, 2)),
                pltpu.SemaphoreType.DMA((2, 2)),
                pltpu.SemaphoreType.DMA((2, 3)),
                pltpu.SemaphoreType.DMA((5,)),
            ],
            compiler_params=pltpu.CompilerParams(
                collective_id=0, has_side_effects=True, vmem_limit_bytes=48 << 20
            ),
        )(slots, slots, adjoint, forward, *consts)

    spec = P(None, None, ("wall", "ckpt"), "mode")
    return jax.shard_map(
        on_device,
        mesh=mesh,
        in_specs=(spec, P("ckpt", None, "wall", "mode"), P("mode")),
        out_specs=spec,
        check_vma=False,
    )
```

```python
import functools

import jax
import jax.numpy as jnp
import numpy as np
from jax import lax
from jax.experimental import pallas as pl
from jax.experimental.pallas import tpu as pltpu
from jax.sharding import PartitionSpec as P

NF = 64
NK = 64
NY = 1024
PEERS = 32
ROWS = 256
F32 = jnp.float32
BF16 = jnp.bfloat16
MESH = pl.DeviceIdType.MESH

IN = {2: 0, 0: 1, 3: 4, 1: 5, 4: 6}
F_OWN, F_OTHER, MID, BACK = 2, 3, 7, 8
OUT = {0: 9, 2: 10, 3: 11, 4: 12, 1: 13}
SLOTS = 14


def hi_lo(table):
    hi = table.astype(np.float32).astype(BF16)
    lo = (table - hi.astype(np.float64)).astype(np.float32).astype(BF16)
    return hi, lo


def complex_blocks(cosine, sine):
    return np.stack([np.stack([cosine, -sine]), np.stack([sine, cosine])])


def tables():
    ids = np.arange(64)
    angle = 2.0 * np.pi / 64 * (ids[:, None] * ids[None, :] % 64)
    cosine, sine = np.cos(angle), np.sin(angle)
    blocks = complex_blocks(cosine, sine)
    eye = np.eye(2)
    span = np.einsum("pqzk,ab->zpaqbk", blocks, eye).reshape(256, 256)
    time = np.einsum("pqtg,ab->patbqg", blocks, eye).reshape(256, 256)
    signed = (ids + 32) % 64 - 32
    beta = 2.0 * signed / 64
    lag = ids[:, None] - ids[None, :]
    wave = np.exp(2j * np.pi / 64 * (lag[:, :, None] * ids % 64))
    slope = (-1j / np.sqrt(NY)) * (wave * beta).sum(-1) / 64
    deriv = np.einsum(
        "pqzx,ab->zpaxqb", complex_blocks(slope.real, slope.imag), eye
    ).reshape(256, 256)
    upto = (np.arange(256)[:, None] <= np.arange(256)[None, :]).astype(np.float32)
    return jnp.asarray(
        np.stack(
            [
                *hi_lo(span),
                *hi_lo(time),
                *hi_lo(-time.T / 128),
                *hi_lo(deriv),
                upto.astype(BF16),
                upto.T.astype(BF16),
            ]
        )
    )


def split(x):
    hi = x.astype(BF16)
    return hi, (x - hi.astype(F32)).astype(BF16)


def dot(a, b, ca=1, cb=0):
    return lax.dot_general(a, b, (((ca,), (cb,)), ((), ())), preferred_element_type=F32)


def kernel(
    slots, adj, fwd, consts, out,
    map_v, table, xin, fin, fz, ptab, sb, db, es, eh, tb, ft, ftb, tm, ti, amp, phys, qs, stage,
    map_sem, table_sem, load_sem, fload_sem, fz_sem, p_sem, ssem, rsem, es_sem, er_sem, tt_sem, ft_sem, st_sem,
):
    me = lax.axis_index("mode")
    wall, ckpt = lax.axis_index("wall"), lax.axis_index("ckpt")
    mx, my, mc = me // 8, (me // 2) % 4, me % 2
    rank = wall * 2 + ckpt

    at_x = [((mx + a) % 4) * 8 for a in range(4)]
    at_y = [((my + b) % 4) * 2 for b in range(4)]
    at_c = [mc, 1 - mc]
    peers = [
        at_x[a] + at_y[b] + at_c[c] for a in range(4) for b in range(4) for c in range(2)
    ][1:]

    def plane(offset):
        other = (rank + offset) % 4
        return {"wall": other // 2, "ckpt": other % 2}

    bar = pltpu.get_barrier_semaphore()

    for p in peers:
        pl.semaphore_signal(bar, inc=1, device_id={"mode": p}, device_id_type=MESH)
    for o in (1, 2, 3):
        pl.semaphore_signal(bar, inc=1, device_id=plane(o), device_id_type=MESH)

    load_table = [
        pltpu.make_async_copy(consts.at[rows], table.at[rows], table_sem.at[i])
        for i, rows in enumerate((pl.ds(0, 2), pl.ds(2, 8)))
    ]
    load_table[0].start()
    span_h, span_l, time_h, time_l, inv_h, inv_l, der_h, der_l, upper, lower = (
        table.at[i] for i in range(10)
    )

    load_map = pltpu.make_async_copy(slots, map_v, map_sem)
    loads = {}
    for c in (2, 0, 3, 4, 1):
        loads[c] = pltpu.make_async_copy(adj.at[:, c], xin.at[c], load_sem.at[c])
        loads[c].start()
        if c == 2:
            load_map.start()
    load_f = pltpu.make_async_copy(
        fwd.at[0, :, pl.ds(ckpt * ROWS, ROWS)], fin, fload_sem
    )
    load_f.start()
    load_table[1].start()

    def exchange(k, value):
        sb[k] = value.reshape(PEERS, 8, ROWS)
        send(k)

    def send(k):
        for p in peers:
            pltpu.make_async_remote_copy(
                sb.at[k, p], db.at[k, me], ssem.at[k], rsem.at[k],
                device_id={"mode": p}, device_id_type=MESH,
            ).start()
        db[k, me] = sb[k, me]

    def whole(k):
        n = pl.ds(0, PEERS - 1)
        return pltpu.make_async_remote_copy(
            sb.at[k, n], db.at[k, n], ssem.at[k], rsem.at[k],
            device_id={"mode": peers[0]}, device_id_type=MESH,
        )

    def arrived(k):
        whole(k).wait_recv()
        return db[k].reshape(ROWS, ROWS)

    def dot3(ah, al, x, cb=0):
        xh, xl = split(x)
        return dot(ah[...], xh, 1, cb) + dot(ah[...], xl, 1, cb) + dot(al[...], xh, 1, cb)

    def to_span(real, imag):
        return dot3(span_h, span_l, jnp.concatenate([real, imag], 1), 1)

    def send_field(c):
        loads[c].wait()
        exchange(IN[c], to_span(xin[c, 0], xin[c, 1]))

    load_table[0].wait()
    loads[2].wait()
    sb[IN[2]] = to_span(xin[2, 0], xin[2, 1]).reshape(PEERS, 8, ROWS)
    load_map.wait()

    pl.semaphore_wait(bar, PEERS - 1 + 3)

    send_fz = pltpu.make_async_remote_copy(
        fwd.at[0, :, pl.ds((1 - ckpt) * ROWS, ROWS)], fz, fz_sem.at[0], fz_sem.at[1],
        device_id={"ckpt": 1 - ckpt}, device_id_type=MESH,
    )
    send_fz.start()
    send(IN[2])
    for p in peers:
        pltpu.make_async_remote_copy(
            map_v, ptab.at[me], p_sem.at[0], p_sem.at[1],
            device_id={"mode": p}, device_id_type=MESH,
        ).start()
    ptab[me] = map_v[...]
    send_field(0)
    load_f.wait()
    exchange(F_OWN, to_span(fin[0], fin[1]))
    send_field(3)

    n = pl.ds(0, PEERS - 1)
    wait_p = pltpu.make_async_remote_copy(
        ptab.at[n], ptab.at[n], p_sem.at[0], p_sem.at[1],
        device_id={"mode": peers[0]}, device_id_type=MESH,
    )
    wait_p.wait_recv()
    load_table[1].wait()
    row = lax.broadcasted_iota(jnp.int32, (ROWS, 128), 0)
    lane = lax.broadcasted_iota(jnp.int32, (ROWS, 128), 1)
    held = jnp.broadcast_to(ptab[...], (PEERS, 8, 128)).reshape(ROWS, 128) >> 6
    freq = jnp.where(row % 2 == lane // 64, held, pltpu.roll(held, 64, 1))
    inside = (row % 8) // 2
    onehot = jnp.concatenate(
        [
            jnp.where(inside * 64 + freq == lane + half * 128, 1.0, 0.0)
            for half in (0, 1)
        ],
        1,
    ).astype(BF16)
    tm[0] = dot(time_h[...], onehot, 1, 1).astype(BF16)
    tm[1] = dot(time_l[...], onehot, 1, 1).astype(BF16)
    ti[0] = dot(onehot, inv_h[...]).astype(BF16)
    ti[1] = dot(onehot, inv_l[...]).astype(BF16)
    signed = jnp.where(freq >= 32, freq - 64, freq).astype(F32) * (1.0 / 1024)
    amp[...] = jnp.where((row // 2) % 2 == 0, signed, -signed)

    first, last = lane == 0, lane == 127
    has_low = (rank > 0).astype(F32)
    has_high = (rank < 3).astype(F32)

    def edge_copies(j):
        return [
            pltpu.make_async_remote_copy(
                es.at[j, s], eh.at[j, s], es_sem.at[j, s], er_sem.at[j, s],
                device_id=plane(o), device_id_type=MESH,
            )
            for s, o in ((0, 1), (1, 3))
        ]

    def send_edges(j, x):
        comb = jnp.where(
            last,
            pltpu.roll(x[:, :128], 127, 1),
            jnp.where(first, pltpu.roll(x[:, 128:], 1, 1), 0.0),
        ).T
        es[j, 0] = comb[:8]
        es[j, 1] = comb[120:]
        for copy in edge_copies(j):
            copy.start()

    def smoothed(x, low, high):
        halo = jnp.concatenate([low, jnp.zeros((112, ROWS), F32), high]).T
        xl, xh = x[:, :128], x[:, 128:]
        dl, dh = pltpu.roll(xl, 1, 1), pltpu.roll(xh, 1, 1)
        ul, uh = pltpu.roll(xl, 127, 1), pltpu.roll(xh, 127, 1)
        below = jnp.concatenate([jnp.where(first, halo, dl), jnp.where(first, dl, dh)], 1)
        above = jnp.concatenate([jnp.where(last, uh, ul), jnp.where(last, halo, uh)], 1)
        return x + 0.2 * ((above - 2.0 * x) + below)

    def to_time(x):
        return dot3(tm.at[0], tm.at[1], x)

    def prepare(c, x, j):
        send_edges(j, x)
        amp_phys = to_time(x)
        phys[c] = amp_phys

    def coupled(c, s):
        ar, ai = phys[c, :128], phys[c, 128:]
        fr, fi = phys[5 + s, :128], phys[5 + s, 128:]
        prod = jnp.concatenate([fr * ar + fi * ai, fr * ai - fi * ar])
        return dot3(ti.at[0], ti.at[1], prod)

    def step(c, x, s, j):
        term = coupled(c, s)
        for copy in edge_copies(j):
            copy.wait_recv()
        return smoothed(x, eh[j, 0] * has_low, eh[j, 1] * has_high) + term

    def first_step(c):
        qs[c] = step(c, db[IN[c]].reshape(ROWS, ROWS), 1, c)

    def begin(c):
        prepare(c, arrived(IN[c]), c)

    def again(c):
        prepare(c, qs[c], 5 + c)

    def finish(c):
        exchange(OUT[c], step(c, qs[c], 0, 5 + c))

    begin(2)
    begin(0)
    send_fz.wait_recv()
    exchange(F_OTHER, to_span(fz[0], fz[1]))
    send_field(1)
    phys[5 + ckpt] = to_time(arrived(F_OWN))
    phys[6 - ckpt] = to_time(arrived(F_OTHER))
    first_step(2)
    exchange(MID, qs[2])
    send_field(4)
    first_step(0)
    again(0)
    again(2)
    begin(3)
    begin(1)
    finish(0)
    first_step(3)
    again(3)
    exchange(BACK, dot3(der_h, der_l, arrived(MID)))
    finish(2)
    first_step(1)
    begin(4)
    finish(3)
    first_step(4)
    again(4)

    u1 = qs[0]
    row2 = lax.broadcasted_iota(jnp.int32, (ROWS, ROWS), 0)
    turned = jnp.where(
        (row2 // 2) % 2 == 0, pltpu.roll(u1, ROWS - 2, 0), pltpu.roll(u1, 2, 0)
    )
    source = turned * jnp.concatenate([amp[...], amp[...]], 1) + arrived(BACK)
    sh, sl = split(source)
    running = dot(sh, upper[...]) + dot(sl, upper[...])
    v1 = qs[1] + running
    j = 6
    second = lane == 1
    comb = jnp.where(
        last,
        pltpu.roll(v1[:, :128], 127, 1),
        jnp.where(
            first,
            pltpu.roll(v1[:, 128:], 1, 1),
            jnp.where(second, pltpu.roll(running[:, 128:], 2, 1), 0.0),
        ),
    ).T
    es[j, 0] = comb[:8]
    es[j, 1] = comb[120:]
    for copy in edge_copies(j):
        copy.start()
    totals = [
        pltpu.make_async_remote_copy(
            es.at[j, 0], tb.at[o - 2], tt_sem.at[0, o - 2], tt_sem.at[1, o - 2],
            device_id=plane(o), device_id_type=MESH,
        )
        for o in (2, 3)
    ]
    for copy in totals:
        copy.start()
    mine = comb[:8]
    finish(4)
    for copy in edge_copies(j) + totals:
        copy.wait_recv()
    nearest = eh[j, 0] * has_low
    beyond = tb[0] * (rank > 1).astype(F32) + tb[1] * (rank > 2).astype(F32)
    prefix = (nearest + beyond)[1:2]
    low = nearest + beyond[1:2] * has_low
    high = (eh[j, 1] + (prefix + mine[1:2])) * has_high
    column = jnp.concatenate([jnp.broadcast_to(prefix, (128, ROWS))]).T
    v1 = v1 + jnp.concatenate([column, column], 1)
    phys[1] = to_time(v1)
    exchange(OUT[1], smoothed(v1, low, high) + coupled(1, 0))

    def stores(c):
        return pltpu.make_async_copy(stage.at[:, c], out.at[:, c], st_sem.at[c])

    def to_slots(c):
        xh, xl = split(arrived(OUT[c]))
        return (
            dot(xh, span_h[...], 0, 0) + dot(xl, span_h[...], 0, 0) + dot(xh, span_l[...], 0, 0)
        ) * (1.0 / 64)

    def put(c, x):
        stage[0, c] = x[:, :128]
        stage[1, c] = x[:, 128:]
        stores(c).start()

    u0 = to_slots(0)
    put(0, u0)
    w0 = to_slots(2)
    put(2, w0)
    slot = map_v[...]
    fi, ki = slot >> 6, slot & 63
    alpha = jnp.where(fi >= 32, fi - 64, fi).astype(F32) * (1.0 / 1024)
    beta = jnp.where(ki >= 32, ki - 64, ki).astype(F32) * (1.0 / 1024)
    source = jnp.concatenate(
        [
            alpha * u0[:, 128:] + beta * w0[:, 128:],
            -(alpha * u0[:, :128] + beta * w0[:, :128]),
        ],
        1,
    )
    sh, sl = split(source)
    running = dot(lower[...], sh) + dot(lower[...], sl)
    ft[...] = running[248:]
    finals = [
        pltpu.make_async_remote_copy(
            ft, ftb.at[o - 1], ft_sem.at[0, o - 1], ft_sem.at[1, o - 1],
            device_id=plane(o), device_id_type=MESH,
        )
        for o in (1, 2, 3)
    ]
    for copy in finals:
        copy.start()
    put(3, to_slots(3))
    for copy in finals:
        copy.wait_recv()
    total = (
        ftb[0] * has_low + ftb[1] * (rank > 1).astype(F32) + ftb[2] * (rank > 2).astype(F32)
    )[7:8]
    running = running + total
    put(4, to_slots(4))
    put(1, to_slots(1) + running)

    for c in range(5):
        stores(c).wait()
    send_fz.wait_send()
    wait_p.wait_send()
    for k in range(SLOTS):
        whole(k).wait_send()
    for j in range(10):
        for copy in edge_copies(j):
            copy.wait_send()
    for copy in totals + finals:
        copy.wait_send()


def solution(mesh):
    def on_device(adjoint, forward, mode_map):
        slots = mode_map.reshape(1, 128)
        consts = tables()
        anywhere = pl.BlockSpec(memory_space=pl.ANY)
        return pl.pallas_call(
            kernel,
            out_shape=jax.ShapeDtypeStruct(adjoint.shape, F32),
            in_specs=[pl.BlockSpec(memory_space=pltpu.HBM)] * 4,
            out_specs=anywhere,
            scratch_shapes=[
                pltpu.VMEM((1, 128), jnp.int32),
                pltpu.VMEM((10, ROWS, ROWS), BF16),
                pltpu.VMEM((5, 2, ROWS, 128), F32),
                pltpu.VMEM((2, ROWS, 128), F32),
                pltpu.VMEM((2, ROWS, 128), F32),
                pltpu.VMEM((PEERS, 1, 128), jnp.int32),
                pltpu.VMEM((SLOTS, PEERS, 8, ROWS), F32),
                pltpu.VMEM((SLOTS, PEERS, 8, ROWS), F32),
                pltpu.VMEM((10, 2, 8, ROWS), F32),
                pltpu.VMEM((10, 2, 8, ROWS), F32),
                pltpu.VMEM((2, 8, ROWS), F32),
                pltpu.VMEM((8, ROWS), F32),
                pltpu.VMEM((3, 8, ROWS), F32),
                pltpu.VMEM((2, ROWS, ROWS), BF16),
                pltpu.VMEM((2, ROWS, ROWS), BF16),
                pltpu.VMEM((ROWS, 128), F32),
                pltpu.VMEM((7, ROWS, ROWS), F32),
                pltpu.VMEM((5, ROWS, ROWS), F32),
                pltpu.VMEM((2, 5, ROWS, 128), F32),
                pltpu.SemaphoreType.DMA,
                pltpu.SemaphoreType.DMA((2,)),
                pltpu.SemaphoreType.DMA((5,)),
                pltpu.SemaphoreType.DMA,
                pltpu.SemaphoreType.DMA((2,)),
                pltpu.SemaphoreType.DMA((2,)),
                pltpu.SemaphoreType.DMA((SLOTS,)),
                pltpu.SemaphoreType.DMA((SLOTS,)),
                pltpu.SemaphoreType.DMA((10, 2)),
                pltpu.SemaphoreType.DMA((10, 2)),
                pltpu.SemaphoreType.DMA((2, 2)),
                pltpu.SemaphoreType.DMA((2, 3)),
                pltpu.SemaphoreType.DMA((5,)),
            ],
            compiler_params=pltpu.CompilerParams(
                collective_id=0, has_side_effects=True, vmem_limit_bytes=53400 << 10
            ),
        )(slots, adjoint, forward, consts)

    spec = P(None, None, ("wall", "ckpt"), "mode")
    return jax.shard_map(
        on_device,
        mesh=mesh,
        in_specs=(spec, P("ckpt", None, "wall", "mode"), P("mode")),
        out_specs=spec,
        check_vma=False,
    )
```

```python
import functools

import jax
import jax.numpy as jnp
import numpy as np
from jax import lax
from jax.experimental import pallas as pl
from jax.experimental.pallas import tpu as pltpu
from jax.sharding import PartitionSpec as P

NF = 64
NK = 64
NY = 1024
PEERS = 32
ROWS = 256
F32 = jnp.float32
BF16 = jnp.bfloat16
MESH = pl.DeviceIdType.MESH

IN = {2: 0, 0: 1, 3: 4, 1: 5, 4: 6}
F_OWN, F_OTHER, MID, BACK = 2, 3, 7, 8
OUT = {0: 9, 2: 10, 3: 11, 4: 12, 1: 13}
SLOTS = 14


def hi_lo(table):
    hi = table.astype(np.float32).astype(BF16)
    lo = (table - hi.astype(np.float64)).astype(np.float32).astype(BF16)
    return hi, lo


def complex_blocks(cosine, sine):
    return np.stack([np.stack([cosine, -sine]), np.stack([sine, cosine])])


def tables():
    ids = np.arange(64)
    angle = 2.0 * np.pi / 64 * (ids[:, None] * ids[None, :] % 64)
    cosine, sine = np.cos(angle), np.sin(angle)
    blocks = complex_blocks(cosine, sine)
    eye = np.eye(2)
    span = np.einsum("pqzk,ab->zpaqbk", blocks, eye).reshape(256, 256)
    time = np.einsum("pqtg,ab->patbqg", blocks, eye).reshape(256, 256)
    signed = (ids + 32) % 64 - 32
    beta = 2.0 * signed / 64
    lag = ids[:, None] - ids[None, :]
    wave = np.exp(2j * np.pi / 64 * (lag[:, :, None] * ids % 64))
    slope = (-1j / np.sqrt(NY)) * (wave * beta).sum(-1) / 64
    deriv = np.einsum(
        "pqzx,ab->zpaxqb", complex_blocks(slope.real, slope.imag), eye
    ).reshape(256, 256)
    upto = (np.arange(256)[:, None] <= np.arange(256)[None, :]).astype(np.float32)
    return jnp.asarray(
        np.stack(
            [
                *hi_lo(span),
                *hi_lo(time),
                *hi_lo(-time.T / 128),
                *hi_lo(deriv),
                upto.astype(BF16),
                upto.T.astype(BF16),
            ]
        )
    )


def split(x):
    hi = x.astype(BF16)
    return hi, (x - hi.astype(F32)).astype(BF16)


def dot(a, b, ca=1, cb=0):
    return lax.dot_general(a, b, (((ca,), (cb,)), ((), ())), preferred_element_type=F32)


def kernel(
    slots, adj, fwd, consts, out,
    map_v, table, xin, fin, fz, ptab, sb, db, es, eh, tb, ft, ftb, tm, ti, amp, phys, qs,
    map_sem, table_sem, load_sem, fload_sem, fz_sem, p_sem, ssem, rsem, es_sem, er_sem, tt_sem, ft_sem,
):
    me = lax.axis_index("mode")
    wall, ckpt = lax.axis_index("wall"), lax.axis_index("ckpt")
    mx, my, mc = me // 8, (me // 2) % 4, me % 2
    rank = wall * 2 + ckpt

    at_x = [((mx + a) % 4) * 8 for a in range(4)]
    at_y = [((my + b) % 4) * 2 for b in range(4)]
    at_c = [mc, 1 - mc]
    peers = [
        at_x[a] + at_y[b] + at_c[c] for a in range(4) for b in range(4) for c in range(2)
    ][1:]

    def plane(offset):
        other = (rank + offset) % 4
        return {"wall": other // 2, "ckpt": other % 2}

    bar = pltpu.get_barrier_semaphore()

    for p in peers:
        pl.semaphore_signal(bar, inc=1, device_id={"mode": p}, device_id_type=MESH)
    for o in (1, 2, 3):
        pl.semaphore_signal(bar, inc=1, device_id=plane(o), device_id_type=MESH)

    load_table = [
        pltpu.make_async_copy(consts.at[rows], table.at[rows], table_sem.at[i])
        for i, rows in enumerate((pl.ds(0, 2), pl.ds(2, 8)))
    ]
    load_table[0].start()
    span_h, span_l, time_h, time_l, inv_h, inv_l, der_h, der_l, upper, lower = (
        table.at[i] for i in range(10)
    )

    load_map = pltpu.make_async_copy(slots, map_v, map_sem)
    loads = {}
    for c in (2, 0, 3, 4, 1):
        loads[c] = pltpu.make_async_copy(adj.at[:, c], xin.at[c], load_sem.at[c])
        loads[c].start()
        if c == 2:
            load_map.start()
    load_f = pltpu.make_async_copy(
        fwd.at[0, :, pl.ds(ckpt * ROWS, ROWS)], fin, fload_sem
    )
    load_f.start()
    load_table[1].start()

    def exchange(k, value):
        sb[k] = value.reshape(PEERS, 8, ROWS)
        send(k)

    def send(k):
        for p in peers:
            pltpu.make_async_remote_copy(
                sb.at[k, p], db.at[k, me], ssem.at[k], rsem.at[k],
                device_id={"mode": p}, device_id_type=MESH,
            ).start()
        db[k, me] = sb[k, me]

    def whole(k):
        n = pl.ds(0, PEERS - 1)
        return pltpu.make_async_remote_copy(
            sb.at[k, n], db.at[k, n], ssem.at[k], rsem.at[k],
            device_id={"mode": peers[0]}, device_id_type=MESH,
        )

    def arrived(k):
        whole(k).wait_recv()
        return db[k].reshape(ROWS, ROWS)

    def dot3(ah, al, x, cb=0):
        xh, xl = split(x)
        return dot(ah[...], xh, 1, cb) + dot(ah[...], xl, 1, cb) + dot(al[...], xh, 1, cb)

    def to_span(real, imag):
        return dot3(span_h, span_l, jnp.concatenate([real, imag], 1), 1)

    def send_field(c):
        loads[c].wait()
        exchange(IN[c], to_span(xin[c, 0], xin[c, 1]))

    load_table[0].wait()
    loads[2].wait()
    sb[IN[2]] = to_span(xin[2, 0], xin[2, 1]).reshape(PEERS, 8, ROWS)
    load_map.wait()

    pl.semaphore_wait(bar, PEERS - 1 + 3)

    send_fz = pltpu.make_async_remote_copy(
        fwd.at[0, :, pl.ds((1 - ckpt) * ROWS, ROWS)], fz, fz_sem.at[0], fz_sem.at[1],
        device_id={"ckpt": 1 - ckpt}, device_id_type=MESH,
    )
    send_fz.start()
    send(IN[2])
    for p in peers:
        pltpu.make_async_remote_copy(
            map_v, ptab.at[me], p_sem.at[0], p_sem.at[1],
            device_id={"mode": p}, device_id_type=MESH,
        ).start()
    ptab[me] = map_v[...]
    send_field(0)
    load_f.wait()
    exchange(F_OWN, to_span(fin[0], fin[1]))
    send_field(3)

    n = pl.ds(0, PEERS - 1)
    wait_p = pltpu.make_async_remote_copy(
        ptab.at[n], ptab.at[n], p_sem.at[0], p_sem.at[1],
        device_id={"mode": peers[0]}, device_id_type=MESH,
    )
    wait_p.wait_recv()
    load_table[1].wait()
    row = lax.broadcasted_iota(jnp.int32, (ROWS, 128), 0)
    lane = lax.broadcasted_iota(jnp.int32, (ROWS, 128), 1)
    held = jnp.broadcast_to(ptab[...], (PEERS, 8, 128)).reshape(ROWS, 128) >> 6
    freq = jnp.where(row % 2 == lane // 64, held, pltpu.roll(held, 64, 1))
    inside = (row % 8) // 2
    onehot = jnp.concatenate(
        [
            jnp.where(inside * 64 + freq == lane + half * 128, 1.0, 0.0)
            for half in (0, 1)
        ],
        1,
    ).astype(BF16)
    tm[0] = dot(time_h[...], onehot, 1, 1).astype(BF16)
    tm[1] = dot(time_l[...], onehot, 1, 1).astype(BF16)
    ti[0] = dot(onehot, inv_h[...]).astype(BF16)
    ti[1] = dot(onehot, inv_l[...]).astype(BF16)
    signed = jnp.where(freq >= 32, freq - 64, freq).astype(F32) * (1.0 / 1024)
    amp[...] = jnp.where((row // 2) % 2 == 0, signed, -signed)

    first, last = lane == 0, lane == 127
    has_low = (rank > 0).astype(F32)
    has_high = (rank < 3).astype(F32)

    def edge_copies(j):
        return [
            pltpu.make_async_remote_copy(
                es.at[j, s], eh.at[j, s], es_sem.at[j, s], er_sem.at[j, s],
                device_id=plane(o), device_id_type=MESH,
            )
            for s, o in ((0, 1), (1, 3))
        ]

    def send_edges(j, x):
        comb = jnp.where(
            last,
            pltpu.roll(x[:, :128], 127, 1),
            jnp.where(first, pltpu.roll(x[:, 128:], 1, 1), 0.0),
        ).T
        es[j, 0] = comb[:8]
        es[j, 1] = comb[120:]
        for copy in edge_copies(j):
            copy.start()

    def smoothed(x, low, high):
        halo = jnp.concatenate([low, jnp.zeros((112, ROWS), F32), high]).T
        xl, xh = x[:, :128], x[:, 128:]
        dl, dh = pltpu.roll(xl, 1, 1), pltpu.roll(xh, 1, 1)
        ul, uh = pltpu.roll(xl, 127, 1), pltpu.roll(xh, 127, 1)
        below = jnp.concatenate([jnp.where(first, halo, dl), jnp.where(first, dl, dh)], 1)
        above = jnp.concatenate([jnp.where(last, uh, ul), jnp.where(last, halo, uh)], 1)
        return x + 0.2 * ((above - 2.0 * x) + below)

    def to_time(x):
        return dot3(tm.at[0], tm.at[1], x)

    def prepare(c, x, j):
        send_edges(j, x)
        amp_phys = to_time(x)
        phys[c] = amp_phys

    def coupled(c, s):
        ar, ai = phys[c, :128], phys[c, 128:]
        fr, fi = phys[5 + s, :128], phys[5 + s, 128:]
        prod = jnp.concatenate([fr * ar + fi * ai, fr * ai - fi * ar])
        return dot3(ti.at[0], ti.at[1], prod)

    def step(c, x, s, j):
        term = coupled(c, s)
        for copy in edge_copies(j):
            copy.wait_recv()
        return smoothed(x, eh[j, 0] * has_low, eh[j, 1] * has_high) + term

    def first_step(c):
        qs[c] = step(c, db[IN[c]].reshape(ROWS, ROWS), 1, c)

    def begin(c):
        prepare(c, arrived(IN[c]), c)

    def again(c):
        prepare(c, qs[c], 5 + c)

    def finish(c):
        exchange(OUT[c], step(c, qs[c], 0, 5 + c))

    begin(2)
    begin(0)
    send_fz.wait_recv()
    exchange(F_OTHER, to_span(fz[0], fz[1]))
    send_field(1)
    send_field(4)
    phys[5 + ckpt] = to_time(arrived(F_OWN))
    phys[6 - ckpt] = to_time(arrived(F_OTHER))
    first_step(2)
    exchange(MID, qs[2])
    first_step(0)
    again(0)
    again(2)
    begin(3)
    begin(1)
    finish(0)
    first_step(3)
    again(3)
    exchange(BACK, dot3(der_h, der_l, arrived(MID)))
    finish(2)
    first_step(1)
    begin(4)
    finish(3)
    first_step(4)
    again(4)

    u1 = qs[0]
    row2 = lax.broadcasted_iota(jnp.int32, (ROWS, ROWS), 0)
    turned = jnp.where(
        (row2 // 2) % 2 == 0, pltpu.roll(u1, ROWS - 2, 0), pltpu.roll(u1, 2, 0)
    )
    source = turned * jnp.concatenate([amp[...], amp[...]], 1) + arrived(BACK)
    sh, sl = split(source)
    running = dot(sh, upper[...]) + dot(sl, upper[...])
    v1 = qs[1] + running
    j = 6
    second = lane == 1
    comb = jnp.where(
        last,
        pltpu.roll(v1[:, :128], 127, 1),
        jnp.where(
            first,
            pltpu.roll(v1[:, 128:], 1, 1),
            jnp.where(second, pltpu.roll(running[:, 128:], 2, 1), 0.0),
        ),
    ).T
    es[j, 0] = comb[:8]
    es[j, 1] = comb[120:]
    for copy in edge_copies(j):
        copy.start()
    totals = [
        pltpu.make_async_remote_copy(
            es.at[j, 0], tb.at[o - 2], tt_sem.at[0, o - 2], tt_sem.at[1, o - 2],
            device_id=plane(o), device_id_type=MESH,
        )
        for o in (2, 3)
    ]
    for copy in totals:
        copy.start()
    mine = comb[:8]
    finish(4)
    for copy in edge_copies(j) + totals:
        copy.wait_recv()
    nearest = eh[j, 0] * has_low
    beyond = tb[0] * (rank > 1).astype(F32) + tb[1] * (rank > 2).astype(F32)
    prefix = (nearest + beyond)[1:2]
    low = nearest + beyond[1:2] * has_low
    high = (eh[j, 1] + (prefix + mine[1:2])) * has_high
    column = jnp.concatenate([jnp.broadcast_to(prefix, (128, ROWS))]).T
    v1 = v1 + jnp.concatenate([column, column], 1)
    phys[1] = to_time(v1)
    exchange(OUT[1], smoothed(v1, low, high) + coupled(1, 0))

    def to_slots(c):
        xh, xl = split(arrived(OUT[c]))
        return (
            dot(xh, span_h[...], 0, 0) + dot(xl, span_h[...], 0, 0) + dot(xh, span_l[...], 0, 0)
        ) * (1.0 / 64)

    def put(c, x):
        out[0, c] = x[:, :128]
        out[1, c] = x[:, 128:]

    u0 = to_slots(0)
    put(0, u0)
    w0 = to_slots(2)
    put(2, w0)
    slot = map_v[...]
    fi, ki = slot >> 6, slot & 63
    alpha = jnp.where(fi >= 32, fi - 64, fi).astype(F32) * (1.0 / 1024)
    beta = jnp.where(ki >= 32, ki - 64, ki).astype(F32) * (1.0 / 1024)
    source = jnp.concatenate(
        [
            alpha * u0[:, 128:] + beta * w0[:, 128:],
            -(alpha * u0[:, :128] + beta * w0[:, :128]),
        ],
        1,
    )
    sh, sl = split(source)
    running = dot(lower[...], sh) + dot(lower[...], sl)
    ft[...] = running[248:]
    finals = [
        pltpu.make_async_remote_copy(
            ft, ftb.at[o - 1], ft_sem.at[0, o - 1], ft_sem.at[1, o - 1],
            device_id=plane(o), device_id_type=MESH,
        )
        for o in (1, 2, 3)
    ]
    for copy in finals:
        copy.start()
    put(3, to_slots(3))
    for copy in finals:
        copy.wait_recv()
    total = (
        ftb[0] * has_low + ftb[1] * (rank > 1).astype(F32) + ftb[2] * (rank > 2).astype(F32)
    )[7:8]
    running = running + total
    put(4, to_slots(4))
    put(1, to_slots(1) + running)

    send_fz.wait_send()
    wait_p.wait_send()
    for k in range(SLOTS):
        whole(k).wait_send()
    for j in range(10):
        for copy in edge_copies(j):
            copy.wait_send()
    for copy in totals + finals:
        copy.wait_send()


def solution(mesh):
    def on_device(adjoint, forward, mode_map):
        slots = mode_map.reshape(1, 128)
        consts = tables()
        return pl.pallas_call(
            kernel,
            out_shape=jax.ShapeDtypeStruct(adjoint.shape, F32),
            in_specs=[pl.BlockSpec(memory_space=pltpu.HBM)] * 4,
            out_specs=pl.BlockSpec(memory_space=pltpu.VMEM),
            scratch_shapes=[
                pltpu.VMEM((1, 128), jnp.int32),
                pltpu.VMEM((10, ROWS, ROWS), BF16),
                pltpu.VMEM((5, 2, ROWS, 128), F32),
                pltpu.VMEM((2, ROWS, 128), F32),
                pltpu.VMEM((2, ROWS, 128), F32),
                pltpu.VMEM((PEERS, 1, 128), jnp.int32),
                pltpu.VMEM((SLOTS, PEERS, 8, ROWS), F32),
                pltpu.VMEM((SLOTS, PEERS, 8, ROWS), F32),
                pltpu.VMEM((10, 2, 8, ROWS), F32),
                pltpu.VMEM((10, 2, 8, ROWS), F32),
                pltpu.VMEM((2, 8, ROWS), F32),
                pltpu.VMEM((8, ROWS), F32),
                pltpu.VMEM((3, 8, ROWS), F32),
                pltpu.VMEM((2, ROWS, ROWS), BF16),
                pltpu.VMEM((2, ROWS, ROWS), BF16),
                pltpu.VMEM((ROWS, 128), F32),
                pltpu.VMEM((7, ROWS, ROWS), F32),
                pltpu.VMEM((5, ROWS, ROWS), F32),
                pltpu.SemaphoreType.DMA,
                pltpu.SemaphoreType.DMA((2,)),
                pltpu.SemaphoreType.DMA((5,)),
                pltpu.SemaphoreType.DMA,
                pltpu.SemaphoreType.DMA((2,)),
                pltpu.SemaphoreType.DMA((2,)),
                pltpu.SemaphoreType.DMA((SLOTS,)),
                pltpu.SemaphoreType.DMA((SLOTS,)),
                pltpu.SemaphoreType.DMA((10, 2)),
                pltpu.SemaphoreType.DMA((10, 2)),
                pltpu.SemaphoreType.DMA((2, 2)),
                pltpu.SemaphoreType.DMA((2, 3)),
            ],
            compiler_params=pltpu.CompilerParams(
                collective_id=0, has_side_effects=True, vmem_limit_bytes=48 << 20
            ),
        )(*(pltpu.with_memory_space_constraint(x, pltpu.HBM) for x in (slots, adjoint, forward, consts)))

    spec = P(None, None, ("wall", "ckpt"), "mode")
    return jax.shard_map(
        on_device,
        mesh=mesh,
        in_specs=(spec, P("ckpt", None, "wall", "mode"), P("mode")),
        out_specs=spec,
        check_vma=False,
    )
```

```python
import functools

import jax
import jax.numpy as jnp
import numpy as np
from jax import lax
from jax.experimental import pallas as pl
from jax.experimental.pallas import tpu as pltpu
from jax.sharding import PartitionSpec as P

NF = 64
NK = 64
NY = 1024
PEERS = 32
ROWS = 256
F32 = jnp.float32
BF16 = jnp.bfloat16
MESH = pl.DeviceIdType.MESH

IN = {2: 0, 0: 1, 3: 4, 1: 5, 4: 6}
F_OWN, F_OTHER, MID, BACK = 2, 3, 7, 8
OUT = {0: 9, 2: 10, 3: 11, 4: 12, 1: 13}
SLOTS = 14


def hi_lo(table):
    hi = table.astype(np.float32).astype(BF16)
    lo = (table - hi.astype(np.float64)).astype(np.float32).astype(BF16)
    return hi, lo


def complex_blocks(cosine, sine):
    return np.stack([np.stack([cosine, -sine]), np.stack([sine, cosine])])


def tables():
    ids = np.arange(64)
    angle = 2.0 * np.pi / 64 * (ids[:, None] * ids[None, :] % 64)
    cosine, sine = np.cos(angle), np.sin(angle)
    blocks = complex_blocks(cosine, sine)
    eye = np.eye(2)
    span = np.einsum("pqzk,ab->zpaqbk", blocks, eye).reshape(256, 256)
    time = np.einsum("pqtg,ab->patbqg", blocks, eye).reshape(256, 256)
    signed = (ids + 32) % 64 - 32
    beta = 2.0 * signed / 64
    lag = ids[:, None] - ids[None, :]
    wave = np.exp(2j * np.pi / 64 * (lag[:, :, None] * ids % 64))
    slope = (-1j / np.sqrt(NY)) * (wave * beta).sum(-1) / 64
    deriv = np.einsum(
        "pqzx,ab->zpaxqb", complex_blocks(slope.real, slope.imag), eye
    ).reshape(256, 256)
    upto = (np.arange(256)[:, None] <= np.arange(256)[None, :]).astype(np.float32)
    return jnp.asarray(
        np.stack(
            [
                *hi_lo(span),
                *hi_lo(time),
                *hi_lo(-time.T / 128),
                *hi_lo(deriv),
                upto.astype(BF16),
                upto.T.astype(BF16),
            ]
        )
    )


def split(x):
    hi = x.astype(BF16)
    return hi, (x - hi.astype(F32)).astype(BF16)


def dot(a, b, ca=1, cb=0):
    return lax.dot_general(a, b, (((ca,), (cb,)), ((), ())), preferred_element_type=F32)


def kernel(
    slots, adj, fwd, consts, out,
    map_v, table, xin, fin, fz, ptab, sb, db, es, eh, tb, ft, ftb, tm, ti, amp, phys, qs,
    map_sem, table_sem, load_sem, fload_sem, fz_sem, p_sem, ssem, rsem, es_sem, er_sem, tt_sem, ft_sem,
):
    me = lax.axis_index("mode")
    wall, ckpt = lax.axis_index("wall"), lax.axis_index("ckpt")
    mx, my, mc = me // 8, (me // 2) % 4, me % 2
    rank = wall * 2 + ckpt

    at_x = [((mx + a) % 4) * 8 for a in range(4)]
    at_y = [((my + b) % 4) * 2 for b in range(4)]
    at_c = [mc, 1 - mc]
    steps = [(a, b, c) for a in range(4) for b in range(4) for c in range(2)][1:]
    steps.sort(key=lambda t: -min(t[0], 4 - t[0]) - min(t[1], 4 - t[1]))
    peers = [at_x[a] + at_y[b] + at_c[c] for a, b, c in steps]

    def plane(offset):
        other = (rank + offset) % 4
        return {"wall": other // 2, "ckpt": other % 2}

    bar = pltpu.get_barrier_semaphore()

    for p in peers:
        pl.semaphore_signal(bar, inc=1, device_id={"mode": p}, device_id_type=MESH)
    for o in (1, 2, 3):
        pl.semaphore_signal(bar, inc=1, device_id=plane(o), device_id_type=MESH)

    load_table = [
        pltpu.make_async_copy(consts.at[rows], table.at[rows], table_sem.at[i])
        for i, rows in enumerate((pl.ds(0, 2), pl.ds(2, 8)))
    ]
    load_table[0].start()
    span_h, span_l, time_h, time_l, inv_h, inv_l, der_h, der_l, upper, lower = (
        table.at[i] for i in range(10)
    )

    load_map = pltpu.make_async_copy(slots, map_v, map_sem)
    loads = {}
    for c in (2, 0, 3, 4, 1):
        loads[c] = pltpu.make_async_copy(adj.at[:, c], xin.at[c], load_sem.at[c])
        loads[c].start()
        if c == 2:
            load_map.start()
    load_f = pltpu.make_async_copy(
        fwd.at[0, :, pl.ds(ckpt * ROWS, ROWS)], fin, fload_sem
    )
    load_f.start()
    load_table[1].start()

    def exchange(k, value):
        sb[k] = value.reshape(PEERS, 8, ROWS)
        send(k)

    def send(k):
        for p in peers:
            pltpu.make_async_remote_copy(
                sb.at[k, p], db.at[k, me], ssem.at[k], rsem.at[k],
                device_id={"mode": p}, device_id_type=MESH,
            ).start()
        db[k, me] = sb[k, me]

    def whole(k):
        n = pl.ds(0, PEERS - 1)
        return pltpu.make_async_remote_copy(
            sb.at[k, n], db.at[k, n], ssem.at[k], rsem.at[k],
            device_id={"mode": peers[0]}, device_id_type=MESH,
        )

    def arrived(k):
        whole(k).wait_recv()
        return db[k].reshape(ROWS, ROWS)

    def dot3(ah, al, x, cb=0):
        xh, xl = split(x)
        return dot(ah[...], xh, 1, cb) + dot(ah[...], xl, 1, cb) + dot(al[...], xh, 1, cb)

    def to_span(real, imag):
        return dot3(span_h, span_l, jnp.concatenate([real, imag], 1), 1)

    def send_field(c):
        loads[c].wait()
        exchange(IN[c], to_span(xin[c, 0], xin[c, 1]))

    load_table[0].wait()
    loads[2].wait()
    sb[IN[2]] = to_span(xin[2, 0], xin[2, 1]).reshape(PEERS, 8, ROWS)
    load_map.wait()

    pl.semaphore_wait(bar, PEERS - 1 + 3)

    send_fz = pltpu.make_async_remote_copy(
        fwd.at[0, :, pl.ds((1 - ckpt) * ROWS, ROWS)], fz, fz_sem.at[0], fz_sem.at[1],
        device_id={"ckpt": 1 - ckpt}, device_id_type=MESH,
    )
    send_fz.start()
    send(IN[2])
    for p in peers:
        pltpu.make_async_remote_copy(
            map_v, ptab.at[me], p_sem.at[0], p_sem.at[1],
            device_id={"mode": p}, device_id_type=MESH,
        ).start()
    ptab[me] = map_v[...]
    send_field(0)
    load_f.wait()
    exchange(F_OWN, to_span(fin[0], fin[1]))
    send_field(3)

    n = pl.ds(0, PEERS - 1)
    wait_p = pltpu.make_async_remote_copy(
        ptab.at[n], ptab.at[n], p_sem.at[0], p_sem.at[1],
        device_id={"mode": peers[0]}, device_id_type=MESH,
    )
    wait_p.wait_recv()
    load_table[1].wait()
    row = lax.broadcasted_iota(jnp.int32, (ROWS, 128), 0)
    lane = lax.broadcasted_iota(jnp.int32, (ROWS, 128), 1)
    held = jnp.broadcast_to(ptab[...], (PEERS, 8, 128)).reshape(ROWS, 128) >> 6
    freq = jnp.where(row % 2 == lane // 64, held, pltpu.roll(held, 64, 1))
    inside = (row % 8) // 2
    onehot = jnp.concatenate(
        [
            jnp.where(inside * 64 + freq == lane + half * 128, 1.0, 0.0)
            for half in (0, 1)
        ],
        1,
    ).astype(BF16)
    tm[0] = dot(time_h[...], onehot, 1, 1).astype(BF16)
    tm[1] = dot(time_l[...], onehot, 1, 1).astype(BF16)
    ti[0] = dot(onehot, inv_h[...]).astype(BF16)
    ti[1] = dot(onehot, inv_l[...]).astype(BF16)
    signed = jnp.where(freq >= 32, freq - 64, freq).astype(F32) * (1.0 / 1024)
    amp[...] = jnp.where((row // 2) % 2 == 0, signed, -signed)

    first, last = lane == 0, lane == 127
    has_low = (rank > 0).astype(F32)
    has_high = (rank < 3).astype(F32)

    def edge_copies(j):
        return [
            pltpu.make_async_remote_copy(
                es.at[j, s], eh.at[j, s], es_sem.at[j, s], er_sem.at[j, s],
                device_id=plane(o), device_id_type=MESH,
            )
            for s, o in ((0, 1), (1, 3))
        ]

    def send_edges(j, x):
        comb = jnp.where(
            last,
            pltpu.roll(x[:, :128], 127, 1),
            jnp.where(first, pltpu.roll(x[:, 128:], 1, 1), 0.0),
        ).T
        es[j, 0] = comb[:8]
        es[j, 1] = comb[120:]
        for copy in edge_copies(j):
            copy.start()

    def smoothed(x, low, high):
        halo = jnp.concatenate([low, jnp.zeros((112, ROWS), F32), high]).T
        xl, xh = x[:, :128], x[:, 128:]
        dl, dh = pltpu.roll(xl, 1, 1), pltpu.roll(xh, 1, 1)
        ul, uh = pltpu.roll(xl, 127, 1), pltpu.roll(xh, 127, 1)
        below = jnp.concatenate([jnp.where(first, halo, dl), jnp.where(first, dl, dh)], 1)
        above = jnp.concatenate([jnp.where(last, uh, ul), jnp.where(last, halo, uh)], 1)
        return x + 0.2 * ((above - 2.0 * x) + below)

    def to_time(x):
        return dot3(tm.at[0], tm.at[1], x)

    def prepare(c, x, j):
        send_edges(j, x)
        amp_phys = to_time(x)
        phys[c] = amp_phys

    def coupled(c, s):
        ar, ai = phys[c, :128], phys[c, 128:]
        fr, fi = phys[5 + s, :128], phys[5 + s, 128:]
        prod = jnp.concatenate([fr * ar + fi * ai, fr * ai - fi * ar])
        return dot3(ti.at[0], ti.at[1], prod)

    def step(c, x, s, j):
        term = coupled(c, s)
        for copy in edge_copies(j):
            copy.wait_recv()
        return smoothed(x, eh[j, 0] * has_low, eh[j, 1] * has_high) + term

    def first_step(c):
        qs[c] = step(c, db[IN[c]].reshape(ROWS, ROWS), 1, c)

    def begin(c):
        prepare(c, arrived(IN[c]), c)

    def again(c):
        prepare(c, qs[c], 5 + c)

    def finish(c):
        exchange(OUT[c], step(c, qs[c], 0, 5 + c))

    begin(2)
    begin(0)
    send_fz.wait_recv()
    exchange(F_OTHER, to_span(fz[0], fz[1]))
    send_field(1)
    send_field(4)
    phys[5 + ckpt] = to_time(arrived(F_OWN))
    phys[6 - ckpt] = to_time(arrived(F_OTHER))
    first_step(2)
    exchange(MID, qs[2])
    first_step(0)
    again(0)
    again(2)
    begin(3)
    begin(1)
    finish(0)
    first_step(3)
    again(3)
    exchange(BACK, dot3(der_h, der_l, arrived(MID)))
    finish(2)
    first_step(1)
    begin(4)
    finish(3)
    first_step(4)
    again(4)

    u1 = qs[0]
    row2 = lax.broadcasted_iota(jnp.int32, (ROWS, ROWS), 0)
    turned = jnp.where(
        (row2 // 2) % 2 == 0, pltpu.roll(u1, ROWS - 2, 0), pltpu.roll(u1, 2, 0)
    )
    source = turned * jnp.concatenate([amp[...], amp[...]], 1) + arrived(BACK)
    sh, sl = split(source)
    running = dot(sh, upper[...]) + dot(sl, upper[...])
    v1 = qs[1] + running
    j = 6
    second = lane == 1
    comb = jnp.where(
        last,
        pltpu.roll(v1[:, :128], 127, 1),
        jnp.where(
            first,
            pltpu.roll(v1[:, 128:], 1, 1),
            jnp.where(second, pltpu.roll(running[:, 128:], 2, 1), 0.0),
        ),
    ).T
    es[j, 0] = comb[:8]
    es[j, 1] = comb[120:]
    for copy in edge_copies(j):
        copy.start()
    totals = [
        pltpu.make_async_remote_copy(
            es.at[j, 0], tb.at[o - 2], tt_sem.at[0, o - 2], tt_sem.at[1, o - 2],
            device_id=plane(o), device_id_type=MESH,
        )
        for o in (2, 3)
    ]
    for copy in totals:
        copy.start()
    mine = comb[:8]
    finish(4)
    for copy in edge_copies(j) + totals:
        copy.wait_recv()
    nearest = eh[j, 0] * has_low
    beyond = tb[0] * (rank > 1).astype(F32) + tb[1] * (rank > 2).astype(F32)
    prefix = (nearest + beyond)[1:2]
    low = nearest + beyond[1:2] * has_low
    high = (eh[j, 1] + (prefix + mine[1:2])) * has_high
    column = jnp.concatenate([jnp.broadcast_to(prefix, (128, ROWS))]).T
    v1 = v1 + jnp.concatenate([column, column], 1)
    phys[1] = to_time(v1)
    exchange(OUT[1], smoothed(v1, low, high) + coupled(1, 0))

    def to_slots(c):
        xh, xl = split(arrived(OUT[c]))
        return (
            dot(xh, span_h[...], 0, 0) + dot(xl, span_h[...], 0, 0) + dot(xh, span_l[...], 0, 0)
        ) * (1.0 / 64)

    def put(c, x):
        out[0, c] = x[:, :128]
        out[1, c] = x[:, 128:]

    u0 = to_slots(0)
    put(0, u0)
    w0 = to_slots(2)
    put(2, w0)
    slot = map_v[...]
    fi, ki = slot >> 6, slot & 63
    alpha = jnp.where(fi >= 32, fi - 64, fi).astype(F32) * (1.0 / 1024)
    beta = jnp.where(ki >= 32, ki - 64, ki).astype(F32) * (1.0 / 1024)
    source = jnp.concatenate(
        [
            alpha * u0[:, 128:] + beta * w0[:, 128:],
            -(alpha * u0[:, :128] + beta * w0[:, :128]),
        ],
        1,
    )
    sh, sl = split(source)
    running = dot(lower[...], sh) + dot(lower[...], sl)
    ft[...] = running[248:]
    finals = [
        pltpu.make_async_remote_copy(
            ft, ftb.at[o - 1], ft_sem.at[0, o - 1], ft_sem.at[1, o - 1],
            device_id=plane(o), device_id_type=MESH,
        )
        for o in (1, 2, 3)
    ]
    for copy in finals:
        copy.start()
    put(3, to_slots(3))
    for copy in finals:
        copy.wait_recv()
    total = (
        ftb[0] * has_low + ftb[1] * (rank > 1).astype(F32) + ftb[2] * (rank > 2).astype(F32)
    )[7:8]
    running = running + total
    put(4, to_slots(4))
    put(1, to_slots(1) + running)

    send_fz.wait_send()
    wait_p.wait_send()
    for k in range(SLOTS):
        whole(k).wait_send()
    for j in range(10):
        for copy in edge_copies(j):
            copy.wait_send()
    for copy in totals + finals:
        copy.wait_send()


def solution(mesh):
    def on_device(adjoint, forward, mode_map):
        slots = mode_map.reshape(1, 128)
        consts = tables()
        return pl.pallas_call(
            kernel,
            out_shape=jax.ShapeDtypeStruct(adjoint.shape, F32),
            in_specs=[pl.BlockSpec(memory_space=pltpu.HBM)] * 4,
            out_specs=pl.BlockSpec(memory_space=pltpu.VMEM),
            scratch_shapes=[
                pltpu.VMEM((1, 128), jnp.int32),
                pltpu.VMEM((10, ROWS, ROWS), BF16),
                pltpu.VMEM((5, 2, ROWS, 128), F32),
                pltpu.VMEM((2, ROWS, 128), F32),
                pltpu.VMEM((2, ROWS, 128), F32),
                pltpu.VMEM((PEERS, 1, 128), jnp.int32),
                pltpu.VMEM((SLOTS, PEERS, 8, ROWS), F32),
                pltpu.VMEM((SLOTS, PEERS, 8, ROWS), F32),
                pltpu.VMEM((10, 2, 8, ROWS), F32),
                pltpu.VMEM((10, 2, 8, ROWS), F32),
                pltpu.VMEM((2, 8, ROWS), F32),
                pltpu.VMEM((8, ROWS), F32),
                pltpu.VMEM((3, 8, ROWS), F32),
                pltpu.VMEM((2, ROWS, ROWS), BF16),
                pltpu.VMEM((2, ROWS, ROWS), BF16),
                pltpu.VMEM((ROWS, 128), F32),
                pltpu.VMEM((7, ROWS, ROWS), F32),
                pltpu.VMEM((5, ROWS, ROWS), F32),
                pltpu.SemaphoreType.DMA,
                pltpu.SemaphoreType.DMA((2,)),
                pltpu.SemaphoreType.DMA((5,)),
                pltpu.SemaphoreType.DMA,
                pltpu.SemaphoreType.DMA((2,)),
                pltpu.SemaphoreType.DMA((2,)),
                pltpu.SemaphoreType.DMA((SLOTS,)),
                pltpu.SemaphoreType.DMA((SLOTS,)),
                pltpu.SemaphoreType.DMA((10, 2)),
                pltpu.SemaphoreType.DMA((10, 2)),
                pltpu.SemaphoreType.DMA((2, 2)),
                pltpu.SemaphoreType.DMA((2, 3)),
            ],
            compiler_params=pltpu.CompilerParams(
                collective_id=0, has_side_effects=True, vmem_limit_bytes=48 << 20
            ),
        )(*(pltpu.with_memory_space_constraint(x, pltpu.HBM) for x in (slots, adjoint, forward, consts)))

    spec = P(None, None, ("wall", "ckpt"), "mode")
    return jax.shard_map(
        on_device,
        mesh=mesh,
        in_specs=(spec, P("ckpt", None, "wall", "mode"), P("mode")),
        out_specs=spec,
        check_vma=False,
    )
```

```python
import functools

import jax
import jax.numpy as jnp
import numpy as np
from jax import lax
from jax.experimental import pallas as pl
from jax.experimental.pallas import tpu as pltpu
from jax.sharding import PartitionSpec as P

NF = 64
NK = 64
NY = 1024
PEERS = 32
ROWS = 256
F32 = jnp.float32
BF16 = jnp.bfloat16
MESH = pl.DeviceIdType.MESH

IN = {2: 0, 0: 1, 3: 4, 1: 5, 4: 6}
F_OWN, F_OTHER, MID, BACK = 2, 3, 7, 8
OUT = {0: 9, 2: 10, 3: 11, 4: 12, 1: 13}
SLOTS = 14


def hi_lo(table):
    hi = table.astype(np.float32).astype(BF16)
    lo = (table - hi.astype(np.float64)).astype(np.float32).astype(BF16)
    return hi, lo


def complex_blocks(cosine, sine):
    return np.stack([np.stack([cosine, -sine]), np.stack([sine, cosine])])


def tables():
    ids = np.arange(64)
    angle = 2.0 * np.pi / 64 * (ids[:, None] * ids[None, :] % 64)
    cosine, sine = np.cos(angle), np.sin(angle)
    blocks = complex_blocks(cosine, sine)
    eye = np.eye(2)
    span = np.einsum("pqzk,ab->zpaqbk", blocks, eye).reshape(256, 256)
    time = np.einsum("pqtg,ab->patbqg", blocks, eye).reshape(256, 256)
    signed = (ids + 32) % 64 - 32
    beta = 2.0 * signed / 64
    lag = ids[:, None] - ids[None, :]
    wave = np.exp(2j * np.pi / 64 * (lag[:, :, None] * ids % 64))
    slope = (-1j / np.sqrt(NY)) * (wave * beta).sum(-1) / 64
    deriv = np.einsum(
        "pqzx,ab->zpaxqb", complex_blocks(slope.real, slope.imag), eye
    ).reshape(256, 256)
    upto = (np.arange(256)[:, None] <= np.arange(256)[None, :]).astype(np.float32)
    return jnp.asarray(
        np.stack(
            [
                *hi_lo(span),
                *hi_lo(time),
                *hi_lo(-time.T / 128),
                *hi_lo(deriv),
                upto.astype(BF16),
                upto.T.astype(BF16),
            ]
        )
    )


def split(x):
    hi = x.astype(BF16)
    return hi, (x - hi.astype(F32)).astype(BF16)


def dot(a, b, ca=1, cb=0):
    return lax.dot_general(a, b, (((ca,), (cb,)), ((), ())), preferred_element_type=F32)


def kernel(
    slots, adj, fwd, consts, out,
    map_v, table, xin, fin, fz, ptab, sb, db, es, eh, tb, ft, ftb, tm, ti, amp, phys, qs,
    map_sem, table_sem, load_sem, fload_sem, fz_sem, p_sem, ssem, rsem, es_sem, er_sem, tt_sem, ft_sem,
):
    me = lax.axis_index("mode")
    wall, ckpt = lax.axis_index("wall"), lax.axis_index("ckpt")
    mx, my, mc = me // 8, (me // 2) % 4, me % 2
    rank = wall * 2 + ckpt

    at_x = [((mx + a) % 4) * 8 for a in range(4)]
    at_y = [((my + b) % 4) * 2 for b in range(4)]
    at_c = [mc, 1 - mc]
    steps = [(a, b, c) for a in range(4) for b in range(4) for c in range(2)][1:]
    steps.sort(key=lambda t: -min(t[0], 4 - t[0]) - min(t[1], 4 - t[1]))
    peers = [at_x[a] + at_y[b] + at_c[c] for a, b, c in steps]

    def plane(offset):
        other = (rank + offset) % 4
        return {"wall": other // 2, "ckpt": other % 2}

    bar = pltpu.get_barrier_semaphore()

    for p in peers:
        pl.semaphore_signal(bar, inc=1, device_id={"mode": p}, device_id_type=MESH)
    for o in (1, 2, 3):
        pl.semaphore_signal(bar, inc=1, device_id=plane(o), device_id_type=MESH)

    load_table = [
        pltpu.make_async_copy(consts.at[rows], table.at[rows], table_sem.at[i])
        for i, rows in enumerate((pl.ds(0, 2), pl.ds(2, 8)))
    ]
    load_table[0].start()
    span_h, span_l, time_h, time_l, inv_h, inv_l, der_h, der_l, upper, lower = (
        table.at[i] for i in range(10)
    )

    load_map = pltpu.make_async_copy(slots, map_v, map_sem)
    loads = {}
    for c in (2, 0, 3, 4, 1):
        loads[c] = pltpu.make_async_copy(adj.at[:, c], xin.at[c], load_sem.at[c])
        loads[c].start()
        if c == 2:
            load_map.start()
    load_f = pltpu.make_async_copy(
        fwd.at[0, :, pl.ds(ckpt * ROWS, ROWS)], fin, fload_sem
    )
    load_f.start()
    load_table[1].start()

    def exchange(k, value):
        sb[k] = value.reshape(PEERS, 8, ROWS)
        send(k)

    def send(k):
        for p in peers:
            pltpu.make_async_remote_copy(
                sb.at[k, p], db.at[k, me], ssem.at[k], rsem.at[k],
                device_id={"mode": p}, device_id_type=MESH,
            ).start()
        db[k, me] = sb[k, me]

    def whole(k):
        n = pl.ds(0, PEERS - 1)
        return pltpu.make_async_remote_copy(
            sb.at[k, n], db.at[k, n], ssem.at[k], rsem.at[k],
            device_id={"mode": peers[0]}, device_id_type=MESH,
        )

    def arrived(k):
        whole(k).wait_recv()
        return db[k].reshape(ROWS, ROWS)

    def dot3(ah, al, x, cb=0):
        xh, xl = split(x)
        return dot(ah[...], xh, 1, cb) + dot(ah[...], xl, 1, cb) + dot(al[...], xh, 1, cb)

    def to_span(real, imag):
        return dot3(span_h, span_l, jnp.concatenate([real, imag], 1), 1)

    def send_field(c):
        loads[c].wait()
        exchange(IN[c], to_span(xin[c, 0], xin[c, 1]))

    load_table[0].wait()
    loads[2].wait()
    sb[IN[2]] = to_span(xin[2, 0], xin[2, 1]).reshape(PEERS, 8, ROWS)
    load_map.wait()

    pl.semaphore_wait(bar, PEERS - 1 + 3)

    send_fz = pltpu.make_async_remote_copy(
        fwd.at[0, :, pl.ds((1 - ckpt) * ROWS, ROWS)], fz, fz_sem.at[0], fz_sem.at[1],
        device_id={"ckpt": 1 - ckpt}, device_id_type=MESH,
    )
    send_fz.start()
    send(IN[2])
    for p in peers:
        pltpu.make_async_remote_copy(
            map_v, ptab.at[me], p_sem.at[0], p_sem.at[1],
            device_id={"mode": p}, device_id_type=MESH,
        ).start()
    ptab[me] = map_v[...]
    send_field(0)
    load_f.wait()
    exchange(F_OWN, to_span(fin[0], fin[1]))
    send_field(3)

    n = pl.ds(0, PEERS - 1)
    wait_p = pltpu.make_async_remote_copy(
        ptab.at[n], ptab.at[n], p_sem.at[0], p_sem.at[1],
        device_id={"mode": peers[0]}, device_id_type=MESH,
    )
    wait_p.wait_recv()
    load_table[1].wait()
    row = lax.broadcasted_iota(jnp.int32, (ROWS, 128), 0)
    lane = lax.broadcasted_iota(jnp.int32, (ROWS, 128), 1)
    held = jnp.broadcast_to(ptab[...], (PEERS, 8, 128)).reshape(ROWS, 128) >> 6
    freq = jnp.where(row % 2 == lane // 64, held, pltpu.roll(held, 64, 1))
    inside = (row % 8) // 2
    onehot = jnp.concatenate(
        [
            jnp.where(inside * 64 + freq == lane + half * 128, 1.0, 0.0)
            for half in (0, 1)
        ],
        1,
    ).astype(BF16)
    tm[0] = dot(time_h[...], onehot, 1, 1).astype(BF16)
    tm[1] = dot(time_l[...], onehot, 1, 1).astype(BF16)
    ti[0] = dot(onehot, inv_h[...]).astype(BF16)
    ti[1] = dot(onehot, inv_l[...]).astype(BF16)
    signed = jnp.where(freq >= 32, freq - 64, freq).astype(F32) * (1.0 / 1024)
    amp[...] = jnp.where((row // 2) % 2 == 0, signed, -signed)

    first, last = lane == 0, lane == 127
    has_low = (rank > 0).astype(F32)
    has_high = (rank < 3).astype(F32)

    def edge_copies(j):
        return [
            pltpu.make_async_remote_copy(
                es.at[j, s], eh.at[j, s], es_sem.at[j, s], er_sem.at[j, s],
                device_id=plane(o), device_id_type=MESH,
            )
            for s, o in ((0, 1), (1, 3))
        ]

    def send_edges(j, x):
        comb = jnp.where(
            last,
            pltpu.roll(x[:, :128], 127, 1),
            jnp.where(first, pltpu.roll(x[:, 128:], 1, 1), 0.0),
        ).T
        es[j, 0] = comb[:8]
        es[j, 1] = comb[120:]
        for copy in edge_copies(j):
            copy.start()

    def smoothed(x, low, high):
        halo = jnp.concatenate([low, jnp.zeros((112, ROWS), F32), high]).T
        xl, xh = x[:, :128], x[:, 128:]
        dl, dh = pltpu.roll(xl, 1, 1), pltpu.roll(xh, 1, 1)
        ul, uh = pltpu.roll(xl, 127, 1), pltpu.roll(xh, 127, 1)
        below = jnp.concatenate([jnp.where(first, halo, dl), jnp.where(first, dl, dh)], 1)
        above = jnp.concatenate([jnp.where(last, uh, ul), jnp.where(last, halo, uh)], 1)
        return x + 0.2 * ((above - 2.0 * x) + below)

    def to_time(x):
        return dot3(tm.at[0], tm.at[1], x)

    def prepare(c, x, j):
        send_edges(j, x)
        amp_phys = to_time(x)
        phys[c] = amp_phys

    def coupled(c, s):
        ar, ai = phys[c, :128], phys[c, 128:]
        fr, fi = phys[5 + s, :128], phys[5 + s, 128:]
        prod = jnp.concatenate([fr * ar + fi * ai, fr * ai - fi * ar])
        return dot3(ti.at[0], ti.at[1], prod)

    def step(c, x, s, j):
        term = coupled(c, s)
        for copy in edge_copies(j):
            copy.wait_recv()
        return smoothed(x, eh[j, 0] * has_low, eh[j, 1] * has_high) + term

    def first_step(c):
        qs[c] = step(c, db[IN[c]].reshape(ROWS, ROWS), 1, c)

    def begin(c):
        prepare(c, arrived(IN[c]), c)

    def again(c):
        prepare(c, qs[c], 5 + c)

    def finish(c):
        exchange(OUT[c], step(c, qs[c], 0, 5 + c))

    begin(2)
    begin(0)
    send_fz.wait_recv()
    exchange(F_OTHER, to_span(fz[0], fz[1]))
    send_field(1)
    send_field(4)
    phys[5 + ckpt] = to_time(arrived(F_OWN))
    phys[6 - ckpt] = to_time(arrived(F_OTHER))
    first_step(0)
    again(0)
    first_step(2)
    exchange(MID, qs[2])
    again(2)
    begin(3)
    begin(1)
    finish(0)
    first_step(3)
    again(3)
    exchange(BACK, dot3(der_h, der_l, arrived(MID)))
    finish(2)
    first_step(1)
    begin(4)
    finish(3)
    first_step(4)
    again(4)

    u1 = qs[0]
    row2 = lax.broadcasted_iota(jnp.int32, (ROWS, ROWS), 0)
    turned = jnp.where(
        (row2 // 2) % 2 == 0, pltpu.roll(u1, ROWS - 2, 0), pltpu.roll(u1, 2, 0)
    )
    source = turned * jnp.concatenate([amp[...], amp[...]], 1) + arrived(BACK)
    sh, sl = split(source)
    running = dot(sh, upper[...]) + dot(sl, upper[...])
    v1 = qs[1] + running
    j = 6
    second = lane == 1
    comb = jnp.where(
        last,
        pltpu.roll(v1[:, :128], 127, 1),
        jnp.where(
            first,
            pltpu.roll(v1[:, 128:], 1, 1),
            jnp.where(second, pltpu.roll(running[:, 128:], 2, 1), 0.0),
        ),
    ).T
    es[j, 0] = comb[:8]
    es[j, 1] = comb[120:]
    for copy in edge_copies(j):
        copy.start()
    totals = [
        pltpu.make_async_remote_copy(
            es.at[j, 0], tb.at[o - 2], tt_sem.at[0, o - 2], tt_sem.at[1, o - 2],
            device_id=plane(o), device_id_type=MESH,
        )
        for o in (2, 3)
    ]
    for copy in totals:
        copy.start()
    mine = comb[:8]
    finish(4)
    for copy in edge_copies(j) + totals:
        copy.wait_recv()
    nearest = eh[j, 0] * has_low
    beyond = tb[0] * (rank > 1).astype(F32) + tb[1] * (rank > 2).astype(F32)
    prefix = (nearest + beyond)[1:2]
    low = nearest + beyond[1:2] * has_low
    high = (eh[j, 1] + (prefix + mine[1:2])) * has_high
    column = jnp.concatenate([jnp.broadcast_to(prefix, (128, ROWS))]).T
    v1 = v1 + jnp.concatenate([column, column], 1)
    phys[1] = to_time(v1)
    exchange(OUT[1], smoothed(v1, low, high) + coupled(1, 0))

    def to_slots(c):
        xh, xl = split(arrived(OUT[c]))
        return (
            dot(xh, span_h[...], 0, 0) + dot(xl, span_h[...], 0, 0) + dot(xh, span_l[...], 0, 0)
        ) * (1.0 / 64)

    def put(c, x):
        out[0, c] = x[:, :128]
        out[1, c] = x[:, 128:]

    u0 = to_slots(0)
    put(0, u0)
    w0 = to_slots(2)
    put(2, w0)
    slot = map_v[...]
    fi, ki = slot >> 6, slot & 63
    alpha = jnp.where(fi >= 32, fi - 64, fi).astype(F32) * (1.0 / 1024)
    beta = jnp.where(ki >= 32, ki - 64, ki).astype(F32) * (1.0 / 1024)
    source = jnp.concatenate(
        [
            alpha * u0[:, 128:] + beta * w0[:, 128:],
            -(alpha * u0[:, :128] + beta * w0[:, :128]),
        ],
        1,
    )
    sh, sl = split(source)
    running = dot(lower[...], sh) + dot(lower[...], sl)
    ft[...] = running[248:]
    finals = [
        pltpu.make_async_remote_copy(
            ft, ftb.at[o - 1], ft_sem.at[0, o - 1], ft_sem.at[1, o - 1],
            device_id=plane(o), device_id_type=MESH,
        )
        for o in (1, 2, 3)
    ]
    for copy in finals:
        copy.start()
    put(3, to_slots(3))
    for copy in finals:
        copy.wait_recv()
    total = (
        ftb[0] * has_low + ftb[1] * (rank > 1).astype(F32) + ftb[2] * (rank > 2).astype(F32)
    )[7:8]
    running = running + total
    put(4, to_slots(4))
    put(1, to_slots(1) + running)

    send_fz.wait_send()
    wait_p.wait_send()
    for k in range(SLOTS):
        whole(k).wait_send()
    for j in range(10):
        for copy in edge_copies(j):
            copy.wait_send()
    for copy in totals + finals:
        copy.wait_send()


def solution(mesh):
    def on_device(adjoint, forward, mode_map):
        slots = mode_map.reshape(1, 128)
        consts = tables()
        return pl.pallas_call(
            kernel,
            out_shape=jax.ShapeDtypeStruct(adjoint.shape, F32),
            in_specs=[pl.BlockSpec(memory_space=pltpu.HBM)] * 4,
            out_specs=pl.BlockSpec(memory_space=pltpu.VMEM),
            scratch_shapes=[
                pltpu.VMEM((1, 128), jnp.int32),
                pltpu.VMEM((10, ROWS, ROWS), BF16),
                pltpu.VMEM((5, 2, ROWS, 128), F32),
                pltpu.VMEM((2, ROWS, 128), F32),
                pltpu.VMEM((2, ROWS, 128), F32),
                pltpu.VMEM((PEERS, 1, 128), jnp.int32),
                pltpu.VMEM((SLOTS, PEERS, 8, ROWS), F32),
                pltpu.VMEM((SLOTS, PEERS, 8, ROWS), F32),
                pltpu.VMEM((10, 2, 8, ROWS), F32),
                pltpu.VMEM((10, 2, 8, ROWS), F32),
                pltpu.VMEM((2, 8, ROWS), F32),
                pltpu.VMEM((8, ROWS), F32),
                pltpu.VMEM((3, 8, ROWS), F32),
                pltpu.VMEM((2, ROWS, ROWS), BF16),
                pltpu.VMEM((2, ROWS, ROWS), BF16),
                pltpu.VMEM((ROWS, 128), F32),
                pltpu.VMEM((7, ROWS, ROWS), F32),
                pltpu.VMEM((5, ROWS, ROWS), F32),
                pltpu.SemaphoreType.DMA,
                pltpu.SemaphoreType.DMA((2,)),
                pltpu.SemaphoreType.DMA((5,)),
                pltpu.SemaphoreType.DMA,
                pltpu.SemaphoreType.DMA((2,)),
                pltpu.SemaphoreType.DMA((2,)),
                pltpu.SemaphoreType.DMA((SLOTS,)),
                pltpu.SemaphoreType.DMA((SLOTS,)),
                pltpu.SemaphoreType.DMA((10, 2)),
                pltpu.SemaphoreType.DMA((10, 2)),
                pltpu.SemaphoreType.DMA((2, 2)),
                pltpu.SemaphoreType.DMA((2, 3)),
            ],
            compiler_params=pltpu.CompilerParams(
                collective_id=0, has_side_effects=True, vmem_limit_bytes=48 << 20
            ),
        )(*(pltpu.with_memory_space_constraint(x, pltpu.HBM) for x in (slots, adjoint, forward, consts)))

    spec = P(None, None, ("wall", "ckpt"), "mode")
    return jax.shard_map(
        on_device,
        mesh=mesh,
        in_specs=(spec, P("ckpt", None, "wall", "mode"), P("mode")),
        out_specs=spec,
        check_vma=False,
    )
```
